32 devices in a mesh: groups: 2 (over y), vox: 4 (over z), sub: 2 (over x), map: 2 (over core).
Axes of the slice: x: 2, y: 2, z: 4, core: 2. Of those that a mesh axis runs over, the one named last changes fastest.
Arguments:
- data: bfloat16 [4, 256, 24576], P('groups', 'map', ('vox', 'sub')), parts along dimension 0, may hold values from -8 to 8
- maps: bfloat16 [400, 24576], P('groups', ('vox', 'sub')), parts along dimension 0, may hold values from -8 to 8
- neighbours: int32 [192, 4], P(('vox', 'sub')), may hold values from 0 to 191, as said below
- weights: float32 [4, 24576], P(None, ('vox', 'sub')), may hold values from 0.1 to 0.6
- noise_labels: int32 [128], P('groups'), parts along dimension 0, may hold values from 0 to 199, as said below
Outputs:
- clean: bfloat16 [4, 256, 24576], P('groups', 'map', ('vox', 'sub')), parts along dimension 0
The draws below stay inside these ranges and needn't reach their ends.
There are 2 independent parts, one for each index of `groups`. The reference program is written for one: setup_inputs(seed, part) draws one part's arguments, and reference() takes and returns one part's arrays. A program takes and returns all parts, laid end to end along the dimension named above; an argument that names none is the same for every part. Nothing has to cross between parts.
Inputs may be any that keep to these rules, and one draw needn't show every extreme that they name: `neighbours`: every entry is within 1 of its own block index; each block lists one neighbour 1 above and one 1 below, cut at the ends of the voxel range. `noise_labels`: distinct component indices.
All inputs are finite; a program needn't handle non-finite values.
Results may differ from the reference program's by a relative error of at most 0.0008.
The reference program's roundings to bfloat16 on the way (of `smoothed` and `noise_beta`) count: a program that leaves them out, or rounds other values in their place, can miss the bound.
Values may be sent and summed in bfloat16 or wider, within the bound.
No kernel may reach another device: no remote copies, remote signals or barrier semaphores. Data moves between devices by JAX's collectives and lax.ppermute only.
A program may use at most 64 MiB of HBM per device.

```python
import math
import jax
import jax.numpy as jnp
from jax import lax

COMP = 200
NOISE = 64
SUBJ = 2
VOXBLK = 128
NEIGHBOUR_SLOTS = 4
NEIGHBOUR_REACH = 1
FRAMES = 256
VOXEL_BLOCKS = 192
VOXEL_COUNT = 24576


def joint_fields(key):
    key_base = jax.random.fold_in(key, 11)
    key_left = jax.random.fold_in(key, 13)
    key_right = jax.random.fold_in(key, 14)
    key_course = jax.random.fold_in(key, 15)
    key_noise = jax.random.fold_in(key, 16)
    base = jax.random.normal(key_base, (COMP, VOXEL_COUNT), jnp.float32)
    scale = jnp.ones((COMP, 1), jnp.float32)
    common = 0.5 * jax.random.normal(key_left, (1, VOXEL_COUNT), jnp.float32) * jax.random.normal(key_right, (COMP, 1), jnp.float32)
    maps = jnp.clip(base + common, -8.0, 8.0).astype(jnp.bfloat16)
    courses = jax.random.normal(key_course, (SUBJ, COMP, FRAMES), jnp.float32) / (math.sqrt(COMP) * scale[None])
    signal = jnp.einsum('cv,scf->sfv', maps.astype(jnp.float32), courses)
    noise = 0.5 * jax.random.normal(key_noise, (SUBJ, FRAMES, VOXEL_COUNT), jnp.float32)
    data = jnp.clip(signal + noise, -8.0, 8.0).astype(jnp.bfloat16)
    return (maps, data)


def draw_maps(key, part):
    return joint_fields(key)[0]


def draw_data(key, part):
    return joint_fields(key)[1]


def draw_neighbours(key, part):
    block_offsets = jax.random.randint(jax.random.fold_in(key, 21), (VOXEL_BLOCKS, NEIGHBOUR_SLOTS), -NEIGHBOUR_REACH, NEIGHBOUR_REACH + 1)
    block_offsets = block_offsets.at[:, 0].set(NEIGHBOUR_REACH).at[:, 1].set(-NEIGHBOUR_REACH)
    own = jnp.arange(VOXEL_BLOCKS, dtype=jnp.int32)[:, None]
    return jnp.clip(own + block_offsets, 0, VOXEL_BLOCKS - 1).astype(jnp.int32)


def draw_noise_labels(key, part):
    order = jax.random.permutation(jax.random.fold_in(key, 31), COMP)
    return order[:NOISE].astype(jnp.int32)


def level_of(rng, extent, cuts, smallest, high):
    def one(dim, parts):
        draws = jax.random.uniform(jax.random.fold_in(jax.random.fold_in(rng, 6), dim), (parts,), jnp.float32, smallest / len(cuts), high / len(cuts))
        return jnp.repeat(jnp.exp(draws), extent[dim] // parts).reshape((-1,) + (1,) * (len(extent) - dim - 1))

    loudness = one(*cuts[0])
    for cut in cuts[1:]:
        loudness = loudness * one(*cut)
    return loudness


def setup_inputs(seed: int = 0, part: int = 0) -> dict:
    seeds = jax.random.split(jax.random.key(seed), 6)
    part_splits = jax.random.split(jax.random.fold_in(seeds[5], part), 6)
    return {
        "data": draw_data(jax.random.fold_in(jax.random.fold_in(seeds[5], part), 71), part),
        "maps": draw_maps(jax.random.fold_in(jax.random.fold_in(seeds[5], part), 71), part),
        "neighbours": draw_neighbours(jax.random.fold_in(seeds[5], 71), part),
        "weights": jnp.clip(jnp.exp(math.log(0.6) - 1.7917595 * jax.random.uniform(seeds[3], (NEIGHBOUR_SLOTS, VOXEL_COUNT), jnp.float32) ** level_of(seeds[3], (NEIGHBOUR_SLOTS, VOXEL_COUNT), ((1, 8),), -0.2, 0.2)), 0.1, 0.6),
        "noise_labels": draw_noise_labels(jax.random.fold_in(jax.random.fold_in(seeds[5], part), 71), part),
    }


def solve_gram(gram, rhs):
    lower = jnp.linalg.cholesky(gram)
    half = lax.linalg.triangular_solve(lower, rhs, left_side=True, lower=True)
    return lax.linalg.triangular_solve(lower, half, left_side=True, lower=True, transpose_a=True)

def subject_smoothing(frames, neighbours, weights):
    blocks = frames.astype(jnp.float32).reshape(frames.shape[0], VOXEL_BLOCKS, VOXBLK)
    total = blocks
    for neighbour_slot in range(NEIGHBOUR_SLOTS):
        picked = jnp.take(blocks, neighbours[:, neighbour_slot], axis=1)
        total = total + weights[neighbour_slot].reshape(VOXEL_BLOCKS, VOXBLK) * picked
    return total.reshape(frames.shape[0], VOXEL_COUNT).astype(jnp.bfloat16)

def reference(data, maps, neighbours, weights, noise_labels):
    smoothed = lax.map(lambda frames: subject_smoothing(frames, neighbours, weights), data)
    gram = jnp.dot(maps.astype(jnp.float32), maps.T.astype(jnp.float32), preferred_element_type=jnp.float32)
    proj = lax.map(lambda frames: jnp.dot(maps.astype(jnp.float32), frames.T.astype(jnp.float32), preferred_element_type=jnp.float32), smoothed)
    rhs = jnp.transpose(proj, (1, 0, 2)).reshape(COMP, SUBJ * FRAMES)
    beta = solve_gram(gram, rhs)
    noise_beta = jnp.take(beta, noise_labels, axis=0).astype(jnp.bfloat16)
    noise_maps = jnp.take(maps, noise_labels, axis=0)
    courses = jnp.transpose(noise_beta.reshape(NOISE, SUBJ, FRAMES), (1, 0, 2))

    def clean_subject(pair):
        frames, course = pair
        fitted = jnp.dot(course.T.astype(jnp.float32), noise_maps.astype(jnp.float32), preferred_element_type=jnp.float32)
        return (frames.astype(jnp.float32) - fitted).astype(jnp.bfloat16)
    return lax.map(clean_subject, (smoothed, courses))
```

```python
import functools

import jax
import jax.numpy as jnp
from jax import lax
from jax.experimental import pallas as pl
from jax.experimental.pallas import tpu as pltpu
from jax.sharding import PartitionSpec as P

VOXBLK = 128
NEIGHBOUR_REACH = 1
LANES = 128
PANEL = 16
EXACT = lax.Precision.HIGHEST
VMEM = pl.BlockSpec(memory_space=pltpu.VMEM)
SMEM = pl.BlockSpec(memory_space=pltpu.SMEM)


def dot(a, b, a_dim, b_dim, precision=None):
    return lax.dot_general(
        a, b, (((a_dim,), (b_dim,)), ((), ())), precision=precision, preferred_element_type=jnp.float32
    )


def cost(flops, read):
    return pl.CostEstimate(flops=flops, bytes_accessed=read, transcendentals=0)


def gram_kernel(core_ref, labels_ref, maps_ref, ordered_ref, half_ref):
    comps = maps_ref.shape[0]
    noise = labels_ref.shape[1]
    labels = labels_ref[...]
    comp = lax.broadcasted_iota(jnp.int32, (comps, noise), 0)
    slot = lax.broadcasted_iota(jnp.int32, (comps, noise), 1)
    hit = labels == comp
    is_noise = jnp.sum(jnp.where(hit, 1.0, 0.0), axis=1, keepdims=True)
    noise_place = jnp.sum(jnp.where(hit, (slot + (comps - noise)).astype(jnp.float32), 0.0), axis=1, keepdims=True)
    below = jnp.sum(jnp.where(labels < comp, 1.0, 0.0), axis=1, keepdims=True)
    own = lax.broadcasted_iota(jnp.int32, (comps, 1), 0).astype(jnp.float32)
    place = jnp.where(is_noise > 0.5, noise_place, own - below)
    column = lax.broadcasted_iota(jnp.int32, (comps, comps), 1).astype(jnp.float32)
    order = jnp.where(place == column, 1.0, 0.0).astype(jnp.bfloat16)
    ordered = dot(order, maps_ref[...], 0, 0).astype(jnp.bfloat16)
    ordered_ref[...] = ordered
    top = dot(ordered, ordered[:LANES], 1, 1)
    low = dot(ordered[LANES:], ordered[LANES:], 1, 1)
    low = jnp.concatenate([low, jnp.zeros((comps - LANES, 2 * LANES - comps), jnp.float32)], axis=1)
    packed = jnp.concatenate([top, low], axis=0)
    half = packed.shape[0] // 2
    half_ref[...] = jnp.where(core_ref[0] == 0, packed[:half], packed[half:])


def gram(core, labels, maps):
    comps, width = maps.shape
    return pl.pallas_call(
        gram_kernel,
        out_shape=(
            jax.ShapeDtypeStruct((comps, width), jnp.bfloat16),
            jax.ShapeDtypeStruct((comps - LANES // 2, LANES), jnp.float32),
        ),
        in_specs=[SMEM, VMEM, VMEM],
        out_specs=(VMEM, VMEM),
        cost_estimate=cost(4 * comps * comps * width, 4 * comps * width),
        name="gram",
    )(core, labels, maps)


def smooth_kernel(where_ref, near_ref, data_ref, low_ref, high_ref, weights_ref, maps_ref, smooth_ref, keep_ref, send_ref, coef_ref):
    rows, width = data_ref.shape
    slots = weights_ref.shape[0]
    blocks = width // VOXBLK
    first = where_ref[0]
    for b in range(blocks):
        cut = slice(b * VOXBLK, (b + 1) * VOXBLK)
        sums = [jnp.zeros((1, VOXBLK), jnp.float32) for _ in range(3)]
        for slot in range(slots):
            off = near_ref[b, slot] - (first + b)
            w = weights_ref[slot:slot + 1, cut]
            for which in range(3):
                sums[which] = sums[which] + jnp.where(off == which - 1, w, 0.0)
        coef_ref[0:1, cut] = sums[0]
        coef_ref[1:2, cut] = sums[1] + 1.0
        coef_ref[2:3, cut] = sums[2]
    step = 16
    for r in range(0, rows, step):
        x = data_ref[r:r + step, :].astype(jnp.float32)
        low = low_ref[r:r + step, :].astype(jnp.float32)
        high = high_ref[r:r + step, :].astype(jnp.float32)
        left = jnp.concatenate([low, x[:, :width - VOXBLK]], axis=1)
        right = jnp.concatenate([x[:, VOXBLK:], high], axis=1)
        total = x * coef_ref[1:2, :] + left * coef_ref[0:1, :] + right * coef_ref[2:3, :]
        smooth_ref[r:r + step, :] = total.astype(jnp.bfloat16)
    proj = dot(maps_ref[...], smooth_ref[...], 1, 1)
    half = rows // 2
    bit = where_ref[1]
    keep_ref[...] = jnp.where(bit == 0, proj[:, :half], proj[:, half:])
    send_ref[...] = jnp.where(bit == 0, proj[:, half:], proj[:, :half])


def smooth(where, near, data, low, high, weights, maps):
    rows, width = data.shape
    comps = maps.shape[0]
    return pl.pallas_call(
        smooth_kernel,
        out_shape=(
            jax.ShapeDtypeStruct((rows, width), jnp.bfloat16),
            jax.ShapeDtypeStruct((comps, rows // 2), jnp.float32),
            jax.ShapeDtypeStruct((comps, rows // 2), jnp.float32),
        ),
        in_specs=[SMEM, SMEM, VMEM, VMEM, VMEM, VMEM, VMEM],
        out_specs=(VMEM, VMEM, VMEM),
        scratch_shapes=[pltpu.VMEM((3, width), jnp.float32)],
        cost_estimate=cost(2 * comps * rows * width, 4 * rows * width),
        name="smooth",
    )(where, near, data, low, high, weights, maps)


def panels(comps, noise):
    found = []
    for low, high in ((0, comps - noise), (comps - noise, comps)):
        while low < high:
            found.append((low, min(PANEL, high - low)))
            low += PANEL
    return found


def inverse_kernel(noise, core_ref, mine_ref, other_ref, out_ref, a_ref):
    comps = a_ref.shape[0]
    lanes = a_ref.shape[1]
    first = comps - noise
    mine, other = mine_ref[...], other_ref[...]
    packed = jnp.concatenate(
        [jnp.where(core_ref[0] == 0, mine, other), jnp.where(core_ref[0] == 0, other, mine)], axis=0
    )
    cross = packed[LANES:comps]
    a_ref[:, :LANES] = packed[:comps]
    a_ref[LANES:, LANES:] = packed[comps:]
    cross = jnp.concatenate([cross, jnp.zeros((2 * LANES - comps, LANES), jnp.float32)], axis=0)
    a_ref[:LANES, LANES:] = jnp.transpose(cross)
    todo = panels(comps, noise)
    panel = a_ref[0:todo[0][1], :]
    for at, (off, w) in enumerate(todo):
        lane = lax.broadcasted_iota(jnp.int32, (w, lanes), 1)
        sub = lax.broadcasted_iota(jnp.int32, (w, LANES), 0)
        wide = lax.broadcasted_iota(jnp.int32, (w, lanes), 0)
        cols = [jnp.broadcast_to(panel[:, off + j:off + j + 1], (w, LANES)) for j in range(w)]
        for k in range(w):
            pivot = 1.0 / jnp.broadcast_to(cols[k][k:k + 1, :], (w, LANES))
            scaled = jnp.where(sub == k, 0.0, cols[k] * pivot)
            for j in range(k + 1, w):
                row = jnp.broadcast_to(cols[j][k:k + 1, :], (w, LANES))
                cols[j] = jnp.where(sub == k, row * pivot, cols[j] - scaled * row)
            row = jnp.broadcast_to(panel[k:k + 1, :], (w, lanes))
            row = jnp.where(lane == off + k, 1.0, row)
            rest = jnp.where(lane == off + k, 0.0, panel)
            pivot = jnp.concatenate([pivot] * (lanes // LANES), axis=1)
            scaled = jnp.concatenate([scaled] * (lanes // LANES), axis=1)
            panel = jnp.where(wide == k, row * pivot, rest - scaled * row)
        if off >= first:
            a_ref[off:off + w, :] = panel
        after = None
        ranges = []
        if at + 1 < len(todo):
            start, size = todo[at + 1]
            after = a_ref[start:start + size, :]
            lane = lax.broadcasted_iota(jnp.int32, (size, lanes), 1)
            total = jnp.where((lane >= off) & (lane < off + w), 0.0, after)
            for j in range(w):
                col = jnp.broadcast_to(after[:, off + j:off + j + 1], (size, lanes))
                total = total - col * jnp.broadcast_to(panel[j:j + 1, :], (size, lanes))
            after = total
            ranges.append((start + size, comps))
        if off > first:
            ranges.append((first, off))
        for low, high in ranges:
            if low < high:
                block = a_ref[low:high, :]
                lane = lax.broadcasted_iota(jnp.int32, (high - low, lanes), 1)
                taken = dot(block[:, off:off + w], panel, 1, 0, EXACT)
                a_ref[low:high, :] = jnp.where((lane >= off) & (lane < off + w), 0.0, block) - taken
        panel = after
    out_ref[...] = a_ref[first:, :]


def inverse_rows(core, mine, other, noise):
    comps = mine.shape[0] + LANES // 2
    return pl.pallas_call(
        functools.partial(inverse_kernel, noise),
        out_shape=jax.ShapeDtypeStruct((noise, 2 * LANES), jnp.float32),
        in_specs=[SMEM, VMEM, VMEM],
        out_specs=VMEM,
        scratch_shapes=[pltpu.VMEM((comps, 2 * LANES), jnp.float32)],
        cost_estimate=cost(4000000000, 4 * comps * comps),
        name="inverse",
    )(core, mine, other)


def beta_kernel(rows_ref, a_ref, b_ref, out_ref):
    proj = a_ref[...] + b_ref[...]
    out_ref[...] = dot(rows_ref[:, :proj.shape[0]], proj, 1, 0, EXACT).astype(jnp.bfloat16)


def noise_courses(rows, a, b):
    return pl.pallas_call(
        beta_kernel,
        out_shape=jax.ShapeDtypeStruct((rows.shape[0], a.shape[1]), jnp.bfloat16),
        in_specs=[VMEM, VMEM, VMEM],
        out_specs=VMEM,
        cost_estimate=cost(12 * rows.shape[0] * a.shape[0] * a.shape[1], 4 * a.shape[0] * a.shape[1]),
        name="courses",
    )(rows, a, b)


def clean_kernel(where_ref, mine_ref, other_ref, maps_ref, smooth_ref, out_ref):
    noise = mine_ref.shape[0]
    first = maps_ref.shape[0] - noise
    mine, other = mine_ref[...], other_ref[...]
    low = where_ref[1] == 0
    half = mine.shape[1]
    for which in range(2):
        take_mine = low if which == 0 else jnp.logical_not(low)
        course = jnp.where(take_mine, mine, other)
        fitted = dot(course, maps_ref[first:, :], 0, 0)
        cut = slice(which * half, (which + 1) * half)
        out_ref[cut, :] = (smooth_ref[cut, :].astype(jnp.float32) - fitted).astype(jnp.bfloat16)


def clean(where, mine, other, maps, smoothed):
    rows, width = smoothed.shape
    comps = maps.shape[0]
    chunk = width // 4 if width % (4 * LANES) == 0 else width
    return pl.pallas_call(
        clean_kernel,
        out_shape=jax.ShapeDtypeStruct((rows, width), jnp.bfloat16),
        grid=(width // chunk,),
        in_specs=[
            SMEM,
            pl.BlockSpec(mine.shape, lambda i: (0, 0)),
            pl.BlockSpec(mine.shape, lambda i: (0, 0)),
            pl.BlockSpec((comps, chunk), lambda i: (0, i)),
            pl.BlockSpec((rows, chunk), lambda i: (0, i)),
        ],
        out_specs=pl.BlockSpec((rows, chunk), lambda i: (0, i)),
        cost_estimate=cost(2 * mine.shape[0] * rows * width, 4 * rows * width),
        name="clean",
    )(where, mine, other, maps, smoothed)


def swap(value, axis, bit):
    return lax.ppermute(value, axis, [(i, i ^ bit) for i in range(lax.axis_size(axis))])


def bits(axis, start=1):
    while start < lax.axis_size(axis):
        yield start
        start *= 2


def local(data, maps, neighbours, weights, noise_labels):
    subjects, frames, width = data.shape
    rows = subjects * frames
    flat = data.reshape(rows, width)
    line = ("vox", "sub")
    count = lax.axis_size(line)
    edge = NEIGHBOUR_REACH * VOXBLK
    forward = [(i, i + 1) for i in range(count - 1)]
    low = lax.ppermute(flat[:, width - edge:], line, forward)
    high = lax.ppermute(flat[:, :edge], line, [(b, a) for a, b in forward])
    core = lax.axis_index("map").astype(jnp.int32).reshape(1)
    first_block = lax.axis_index(line) * (width // VOXBLK)
    where = jnp.stack([first_block, lax.axis_index("sub") & 1]).astype(jnp.int32)

    ordered, mine = gram(core, noise_labels.reshape(1, -1), maps)
    for bit in bits("sub"):
        mine = mine + swap(mine, "sub", bit)
    smoothed, keep, send = smooth(where, neighbours, flat, low, high, weights, ordered)
    for bit in bits("vox"):
        mine = mine + swap(mine, "vox", bit)
    other = swap(mine, "map", 1)

    got = swap(send, "sub", 1)
    steps = [("sub", bit) for bit in bits("sub", 2)] + [("vox", bit) for bit in bits("vox")]
    for axis, bit in steps:
        keep = keep + got
        got = swap(keep, axis, bit)
    rows_of_inverse = inverse_rows(core, mine, other, noise_labels.shape[0])
    mine = noise_courses(rows_of_inverse, keep, got)
    other = swap(mine, "sub", 1)
    out = clean(where, mine, other, ordered, smoothed)
    return out.reshape(subjects, frames, width)


def solution(mesh):
    return jax.shard_map(
        local,
        mesh=mesh,
        in_specs=(
            P("groups", "map", ("vox", "sub")),
            P("groups", ("vox", "sub")),
            P(("vox", "sub"), None),
            P(None, ("vox", "sub")),
            P("groups"),
        ),
        out_specs=P("groups", "map", ("vox", "sub")),
        check_vma=False,
    )
```

```python
import functools

import jax
import jax.numpy as jnp
from jax import lax
from jax.experimental import pallas as pl
from jax.experimental.pallas import tpu as pltpu
from jax.sharding import PartitionSpec as P

VOXBLK = 128
NEIGHBOUR_REACH = 1
LANES = 128
PANEL = 16
EXACT = lax.Precision.HIGHEST
VMEM = pl.BlockSpec(memory_space=pltpu.VMEM)
SMEM = pl.BlockSpec(memory_space=pltpu.SMEM)
HBM = pl.BlockSpec(memory_space=pltpu.HBM)


def dot(a, b, a_dim, b_dim, precision=None):
    return lax.dot_general(
        a, b, (((a_dim,), (b_dim,)), ((), ())), precision=precision, preferred_element_type=jnp.float32
    )


def cost(flops, read):
    return pl.CostEstimate(flops=flops, bytes_accessed=read, transcendentals=0)


def room(mebibytes):
    return pltpu.CompilerParams(vmem_limit_bytes=mebibytes << 20)


def on_first_core():
    return lax.axis_index("map") == 0


def chunks_of(width):
    count = 4 if width % (4 * LANES) == 0 else 1
    return [(i, slice(i * (width // count), (i + 1) * (width // count))) for i in range(count)]


def gram_kernel(labels_hbm, maps_hbm, ordered_ref, half_ref, labels_ref, maps_ref, label_sem, sems):
    comps, width = maps_ref.shape
    noise = labels_ref.shape[1]
    parts = chunks_of(width)
    copies = [pltpu.make_async_copy(maps_hbm.at[:, cut], maps_ref.at[:, cut], sems.at[i]) for i, cut in parts]
    first = pltpu.make_async_copy(labels_hbm, labels_ref, label_sem)
    first.start()
    for copy in copies:
        copy.start()
    first.wait()
    labels = labels_ref[...]
    comp = lax.broadcasted_iota(jnp.int32, (comps, noise), 0)
    slot = lax.broadcasted_iota(jnp.int32, (comps, noise), 1)
    hit = labels == comp
    is_noise = jnp.sum(jnp.where(hit, 1.0, 0.0), axis=1, keepdims=True)
    there = (slot + (comps - noise)).astype(jnp.float32)
    noise_place = jnp.sum(jnp.where(hit, there, 0.0), axis=1, keepdims=True)
    below = jnp.sum(jnp.where(labels < comp, 1.0, 0.0), axis=1, keepdims=True)
    own = lax.broadcasted_iota(jnp.int32, (comps, 1), 0).astype(jnp.float32)
    place = jnp.where(is_noise > 0.5, noise_place, own - below)
    place = jnp.transpose(jnp.broadcast_to(place, (comps, LANES)))[0:1]
    row = lax.broadcasted_iota(jnp.int32, (comps, comps), 0).astype(jnp.float32)
    order = jnp.where(place == row, 1.0, 0.0).astype(jnp.bfloat16)
    top = jnp.zeros((comps, LANES), jnp.float32)
    low = jnp.zeros((comps - LANES, comps - LANES), jnp.float32)
    for i, cut in parts:
        copies[i].wait()
        ordered = dot(order, maps_ref[:, cut], 1, 0).astype(jnp.bfloat16)
        ordered_ref[:, cut] = ordered
        top = top + dot(ordered, ordered[:LANES], 1, 1)
        low = low + dot(ordered[LANES:], ordered[LANES:], 1, 1)
    low = jnp.concatenate([low, jnp.zeros((comps - LANES, 2 * LANES - comps), jnp.float32)], axis=1)
    packed = jnp.concatenate([top, low], axis=0)
    half = half_ref.shape[0]
    half_ref[...] = jnp.where(on_first_core(), packed[:half], packed[half:])


def gram(labels, maps):
    comps, width = maps.shape
    return pl.pallas_call(
        gram_kernel,
        out_shape=(
            jax.ShapeDtypeStruct((comps, width), jnp.bfloat16),
            jax.ShapeDtypeStruct((comps - LANES // 2, LANES), jnp.float32),
        ),
        in_specs=[HBM, HBM],
        out_specs=(VMEM, VMEM),
        scratch_shapes=[
            pltpu.VMEM(labels.shape, jnp.int32),
            pltpu.VMEM((comps, width), jnp.bfloat16),
            pltpu.SemaphoreType.DMA,
            pltpu.SemaphoreType.DMA((len(chunks_of(width)),)),
        ],
        compiler_params=room(8),
        cost_estimate=cost(4 * comps * comps * width, 4 * comps * width),
        name="gram",
    )(labels, maps)


def smooth_kernel(near_ref, data_ref, pair_ref, next_ref, weights_ref, maps_ref, smooth_ref, keep_ref, send_ref, coef_ref):
    rows, width = data_ref.shape
    slots = weights_ref.shape[0]
    blocks = width // VOXBLK
    first = lax.axis_index(("vox", "sub")) * blocks
    for b in range(blocks):
        cut = slice(b * VOXBLK, (b + 1) * VOXBLK)
        sums = [jnp.zeros((1, VOXBLK), jnp.float32) for _ in range(3)]
        for slot in range(slots):
            off = near_ref[slot, b] - (first + b)
            w = weights_ref[slot:slot + 1, cut]
            for which in range(3):
                sums[which] = sums[which] + jnp.where(off == which - 1, w, 0.0)
        coef_ref[0:1, cut] = sums[0]
        coef_ref[1:2, cut] = sums[1] + 1.0
        coef_ref[2:3, cut] = sums[2]
    step = 16
    odd = lax.axis_index(("vox", "sub")) & 1 == 1
    for r in range(0, rows, step):
        x = data_ref[r:r + step, :].astype(jnp.float32)
        pair = pair_ref[r:r + step, :].astype(jnp.float32)
        far = next_ref[r:r + step, :].astype(jnp.float32)
        low = jnp.where(odd, pair, far)
        high = jnp.where(odd, far, pair)
        left = jnp.concatenate([low, x[:, :width - VOXBLK]], axis=1)
        right = jnp.concatenate([x[:, VOXBLK:], high], axis=1)
        total = x * coef_ref[1:2, :] + left * coef_ref[0:1, :] + right * coef_ref[2:3, :]
        smooth_ref[r:r + step, :] = total.astype(jnp.bfloat16)
    proj = dot(maps_ref[...], smooth_ref[...], 1, 1)
    half = rows // 2
    bit = lax.axis_index("sub") & 1
    keep_ref[...] = jnp.where(bit == 0, proj[:, :half], proj[:, half:])
    send_ref[...] = jnp.where(bit == 0, proj[:, half:], proj[:, :half])


def smooth(near, data, pair, far, weights, maps):
    rows, width = data.shape
    comps = maps.shape[0]
    return pl.pallas_call(
        smooth_kernel,
        out_shape=(
            jax.ShapeDtypeStruct((rows, width), jnp.bfloat16),
            jax.ShapeDtypeStruct((comps, rows // 2), jnp.float32),
            jax.ShapeDtypeStruct((comps, rows // 2), jnp.float32),
        ),
        in_specs=[SMEM, VMEM, VMEM, VMEM, VMEM, VMEM],
        out_specs=(VMEM, VMEM, VMEM),
        scratch_shapes=[pltpu.VMEM((3, width), jnp.float32)],
        cost_estimate=cost(2 * comps * rows * width, 4 * rows * width),
        compiler_params=room(16),
        name="smooth",
    )(near, data, pair, far, weights, maps)


def panels(low, high):
    return [(at, min(PANEL, high - at)) for at in range(low, high, PANEL)]


def eliminate(a_ref, base, comps, todo, keep):
    lanes = a_ref.shape[1]
    first = todo[0][0]
    panel = a_ref[first - base:first - base + todo[0][1], :]
    for at, (off, w) in enumerate(todo):
        lane = lax.broadcasted_iota(jnp.int32, (w, lanes), 1)
        sub = lax.broadcasted_iota(jnp.int32, (w, LANES), 0)
        wide = lax.broadcasted_iota(jnp.int32, (w, lanes), 0)
        cols = [jnp.broadcast_to(panel[:, off + j:off + j + 1], (w, LANES)) for j in range(w)]
        for k in range(w):
            pivot = 1.0 / jnp.broadcast_to(cols[k][k:k + 1, :], (w, LANES))
            scaled = jnp.where(sub == k, 0.0, cols[k] * pivot)
            for j in range(k + 1, w):
                row = jnp.broadcast_to(cols[j][k:k + 1, :], (w, LANES))
                cols[j] = jnp.where(sub == k, row * pivot, cols[j] - scaled * row)
            row = jnp.broadcast_to(panel[k:k + 1, :], (w, lanes))
            row = jnp.where(lane == off + k, 1.0, row)
            rest = jnp.where(lane == off + k, 0.0, panel)
            pivot = jnp.concatenate([pivot] * (lanes // LANES), axis=1)
            scaled = jnp.concatenate([scaled] * (lanes // LANES), axis=1)
            panel = jnp.where(wide == k, row * pivot, rest - scaled * row)
        if keep:
            a_ref[off - base:off - base + w, :] = panel
        after = None
        ranges = []
        start = off + w
        if at + 1 < len(todo):
            start, size = todo[at + 1]
            after = a_ref[start - base:start - base + size, :]
            lane = lax.broadcasted_iota(jnp.int32, (size, lanes), 1)
            total = jnp.where((lane >= off) & (lane < off + w), 0.0, after)
            for j in range(w):
                col = jnp.broadcast_to(after[:, off + j:off + j + 1], (size, lanes))
                total = total - col * jnp.broadcast_to(panel[j:j + 1, :], (size, lanes))
            after = total
            start += size
        ranges.append((start, comps))
        if keep:
            ranges.append((first, off))
        for low, high in ranges:
            if low < high:
                block = a_ref[low - base:high - base, :]
                lane = lax.broadcasted_iota(jnp.int32, (high - low, lanes), 1)
                taken = dot(block[:, off:off + w], panel, 1, 0, EXACT)
                a_ref[low - base:high - base, :] = jnp.where((lane >= off) & (lane < off + w), 0.0, block) - taken
        panel = after


def signal_kernel(mine_ref, other_ref, out_ref, a_ref):
    comps = a_ref.shape[0]
    first = comps - out_ref.shape[0]
    mine, other = mine_ref[...], other_ref[...]
    ahead = on_first_core()
    packed = jnp.concatenate([jnp.where(ahead, mine, other), jnp.where(ahead, other, mine)], axis=0)
    a_ref[:, :LANES] = packed[:comps]
    a_ref[LANES:, LANES:] = packed[comps:]
    cross = jnp.concatenate([packed[LANES:comps], jnp.zeros((2 * LANES - comps, LANES), jnp.float32)], axis=0)
    a_ref[:LANES, LANES:] = jnp.transpose(cross)
    eliminate(a_ref, 0, comps, panels(0, first), False)
    out_ref[...] = a_ref[first:, :]


def noise_kernel(comps, a_ref, out_ref, b_ref):
    first = comps - out_ref.shape[0]
    b_ref[...] = a_ref[...]
    eliminate(b_ref, first, comps, panels(first, comps), True)
    out_ref[...] = b_ref[...]


def after_signal(a, b, noise):
    comps = a.shape[0] + LANES // 2
    return pl.pallas_call(
        signal_kernel,
        out_shape=jax.ShapeDtypeStruct((noise, 2 * LANES), jnp.float32),
        in_specs=[VMEM, VMEM],
        out_specs=VMEM,
        scratch_shapes=[pltpu.VMEM((comps, 2 * LANES), jnp.float32)],
        compiler_params=room(6),
        cost_estimate=cost(2000000000, 4 * comps * comps),
        name="signal",
    )(a, b)


def inverse_rows(a, comps):
    return pl.pallas_call(
        functools.partial(noise_kernel, comps),
        out_shape=jax.ShapeDtypeStruct(a.shape, jnp.float32),
        in_specs=[VMEM],
        out_specs=VMEM,
        scratch_shapes=[pltpu.VMEM(a.shape, jnp.float32)],
        compiler_params=room(6),
        cost_estimate=cost(1500000000, 4 * comps * comps),
        name="noise",
    )(a)


def course_kernel(rows_ref, *refs):
    out_ref = refs[-1]
    proj = tree([ref[...] for ref in refs[:-1]])
    out_ref[...] = dot(proj, rows_ref[:, :proj.shape[0]], 0, 1, EXACT).astype(jnp.bfloat16)


def noise_courses(rows, parts):
    comps, half = parts[0].shape
    return pl.pallas_call(
        course_kernel,
        out_shape=jax.ShapeDtypeStruct((half, rows.shape[0]), jnp.bfloat16),
        in_specs=[VMEM] * (1 + len(parts)),
        out_specs=VMEM,
        compiler_params=room(4),
        cost_estimate=cost(12 * rows.shape[0] * comps * half, 4 * comps * half),
        name="courses",
    )(rows, *parts)


def clean_kernel(mine_ref, other_ref, maps_ref, smooth_ref, out_hbm, out_ref, sems):
    noise = mine_ref.shape[1]
    comps, width = maps_ref.shape
    mine, other = mine_ref[...], other_ref[...]
    low = lax.axis_index("sub") & 1 == 0
    course = jnp.concatenate([jnp.where(low, mine, other), jnp.where(low, other, mine)], axis=0)
    copies = []
    for i, cut in chunks_of(width):
        fitted = dot(course, maps_ref[comps - noise:, cut], 1, 0)
        out_ref[:, cut] = (smooth_ref[:, cut].astype(jnp.float32) - fitted).astype(jnp.bfloat16)
        copies.append(pltpu.make_async_copy(out_ref.at[:, cut], out_hbm.at[:, cut], sems.at[i]))
        copies[-1].start()
    for copy in copies:
        copy.wait()


def clean(mine, other, maps, smoothed):
    rows, width = smoothed.shape
    return pl.pallas_call(
        clean_kernel,
        out_shape=jax.ShapeDtypeStruct((rows, width), jnp.bfloat16),
        in_specs=[VMEM] * 4,
        out_specs=HBM,
        scratch_shapes=[
            pltpu.VMEM((rows, width), jnp.bfloat16),
            pltpu.SemaphoreType.DMA((len(chunks_of(width)),)),
        ],
        compiler_params=room(12),
        cost_estimate=cost(2 * mine.shape[1] * rows * width, 4 * rows * width),
        name="clean",
    )(mine, other, maps, smoothed)


def swap(value, axis, bit, name):
    with jax.named_scope(name):
        return lax.ppermute(value, axis, [(i, i ^ bit) for i in range(lax.axis_size(axis))])


def tree(parts):
    while len(parts) > 1:
        parts = [parts[i] + parts[i + 1] if i + 1 < len(parts) else parts[i] for i in range(0, len(parts), 2)]
    return parts[0]


def stages(axis, start=1):
    size = lax.axis_size(axis)
    while start < size:
        radix = 4 if size % (4 * start) == 0 else 2
        yield axis, [start * i for i in range(1, radix)]
        start *= radix


def gather_parts(value, steps, name):
    parts = [value]
    for at, (axis, partners) in enumerate(steps):
        value = tree(parts)
        parts = [value] + [swap(value, axis, bit, f"{name}{at}_{bit}") for bit in partners]
    return parts


def local(data, maps, neighbours, weights, noise_labels):
    subjects, frames, width = data.shape
    comps = maps.shape[0]
    flat = data.reshape(subjects * frames, width)
    line = ("vox", "sub")
    count = lax.axis_size(line)
    edge = NEIGHBOUR_REACH * VOXBLK

    even = lax.axis_index(line) % 2 == 0
    upper, lower = width - edge, 0
    to_pair = lax.dynamic_slice_in_dim(flat, jnp.where(even, upper, lower), edge, axis=1)
    to_next = lax.dynamic_slice_in_dim(flat, jnp.where(even, lower, upper), edge, axis=1)
    with jax.named_scope("pair"):
        pair = lax.ppermute(to_pair, line, [(i, i ^ 1) for i in range(count)])
    groups = lax.axis_size("groups")
    ring = []
    for g in range(groups):
        ring += [(g * count + i, g * count + (i + 1 if i % 2 else i - 1)) for i in range(1, count - 1)]
        if groups % 2 == 0:
            ring += [(g * count + i, (g ^ 1) * count + i) for i in (0, count - 1)]
    with jax.named_scope("next"):
        far = lax.ppermute(to_next, ("groups",) + line, ring)

    ordered, half = gram(noise_labels.reshape(1, -1), maps)
    smoothed, keep, send = smooth(neighbours.T, flat, pair, far, weights, ordered)
    mine = tree(gather_parts(half, [*stages("sub"), *stages("vox")], "g"))
    other = swap(mine, "map", 1, "gm")
    rows = inverse_rows(after_signal(mine, other, noise_labels.shape[0]), comps)

    keep = keep + swap(send, "sub", 1, "p")
    parts = gather_parts(keep, [*stages("sub", 2), *stages("vox")], "p")
    mine = noise_courses(rows, parts)
    other = swap(mine, "sub", 1, "last")
    out = clean(mine, other, ordered, smoothed)
    return out.reshape(subjects, frames, width)


def solution(mesh):
    return jax.shard_map(
        local,
        mesh=mesh,
        in_specs=(
            P("groups", "map", ("vox", "sub")),
            P("groups", ("vox", "sub")),
            P(("vox", "sub"), None),
            P(None, ("vox", "sub")),
            P("groups"),
        ),
        out_specs=P("groups", "map", ("vox", "sub")),
        check_vma=False,
    )
```
